32 devices in a mesh: section: 2 (over x), head: 4 (over y, core), dp: 4 (over z).
Axes of the slice: x: 2, y: 2, z: 4, core: 2. Of those that a mesh axis runs over, the one named last changes fastest.
Arguments:
- tokens: bfloat16 [4, 2, 1536, 768], P('dp', None, 'head'), may hold values from -6 to 6
- images: int32 [4, 2, 1536], P('dp'), may hold values from 0 to 5, never falling along the last dimension, each value on 1 to 1024 neighbouring positions
- norm_gain: float32 [2, 2, 768], P('section'), may hold values from 0.5 to 1.5
- norm_shift: float32 [2, 2, 768], P('section'), may hold values from -1.5 to 1.5
- input_bias: float32 [2, 2, 768], P('section', None, 'head'), may hold values from -2.5 to 2.5
- project_in: bfloat16 [2, 3, 768, 768], P('section', None, None, 'head'), may hold values from -0.21875 to 0.21875
- project_out: bfloat16 [2, 768, 768], P('section', 'head'), may hold values from -1.75 to 1.75
- branch_bias: float32 [2, 2, 768], P('section'), may hold values from -1.5 to 1.5
- layer_scale: float32 [2, 2, 768], P('section'), may hold values from 0.5 to 2
- expand_bias: float32 [2, 3072], P('section', 'head'), may hold values from -1.5 to 1.5
- expand_weight: bfloat16 [2, 768, 3072], P('section', None, 'head'), may hold values from -0.21875 to 0.21875
- reduce_weight: bfloat16 [2, 3072, 768], P('section', 'head'), may hold values from -0.109375 to 0.109375
- cotangent: bfloat16 [4, 2, 1536, 768], P('dp', None, 'head'), may hold values from -6 to 6
Outputs:
- final_tokens: bfloat16 [4, 2, 1536, 768], P('dp', 'section', 'head')
- grad_tokens: bfloat16 [4, 2, 1536, 768], P('dp', 'section', 'head')
- grad_norm_gain: float32 [2, 2, 768], P('section')
- grad_norm_shift: float32 [2, 2, 768], P('section')
- grad_input_bias: float32 [2, 2, 768], P('section', None, 'head')
- grad_project_in: float32 [2, 3, 768, 768], P('section', None, None, 'head')
- grad_project_out: float32 [2, 768, 768], P('section', 'head')
- grad_branch_bias: float32 [2, 2, 768], P('section')
- grad_layer_scale: float32 [2, 2, 768], P('section')
- grad_expand_bias: float32 [2, 3072], P('section', 'head')
- grad_expand_weight: float32 [2, 768, 3072], P('section', None, 'head')
- grad_reduce_weight: float32 [2, 3072, 768], P('section', 'head')
The draws below stay inside these ranges and needn't reach their ends.
Inputs may be any that keep to these rules, and one draw needn't show every extreme that they name: `images`: images are whole and contiguous within a slot: numbers never fall along a slot, and every slot holds one image of exactly 1024 tokens beside smaller ones.
All inputs are finite; a program needn't handle non-finite values.
Results may differ from the reference program's by a relative error of at most 0.018.
Values may be sent and summed in bfloat16 or wider, within the bound.
No kernel may reach another device: no remote copies, remote signals or barrier semaphores. Data moves between devices by JAX's collectives and lax.ppermute only.
A program may use at most 192 MiB of HBM per device.

```python
import math
import jax
import jax.numpy as jnp
import numpy as np
from jax import lax

D = 768
HEADS = 12
HEAD_DIM = 64
FF = 3072
SLOT = 1536
MB = 2
IMAGES = 6
LONGEST = 1024
LAYERS = 2
RANKS = 4


def level_of(key, dims, cuts, least, high):
    def one(dim, blocks):
        steps = jax.random.uniform(jax.random.fold_in(jax.random.fold_in(key, 6), dim), (blocks,), jnp.float32, least / len(cuts), high / len(cuts))
        return jnp.repeat(jnp.exp(steps), dims[dim] // blocks).reshape((-1,) + (1,) * (len(dims) - dim - 1))

    factor_of = one(*cuts[0])
    for cut in cuts[1:]:
        factor_of = factor_of * one(*cut)
    return factor_of


def split_up(amount, total, limit, skew):
    loads = [(1 << 20) // math.isqrt(rank ** skew) + 1 for rank in range(2, amount + 1)]
    spare, holding = total - limit - (amount - 1), [1] * (amount - 1)
    while spare > 0:
        candidates = [i for i in range(amount - 1) if holding[i] < limit]
        mass, budget = sum([loads[i] for i in candidates]), spare
        for i in candidates:
            extra = min(limit - holding[i], max(1, budget * loads[i] // mass), spare)
            holding[i] = holding[i] + extra
            spare = spare - extra
    return np.array([limit] + holding)


def ragged(rng, amount, total, limit, skew):
    if amount == 2:
        one = jax.random.randint(rng, (), max(1, total - limit), min(limit, total - 1) + 1)
        return jnp.stack([one, total - one])
    lengths = jnp.asarray(split_up(amount, total, limit, skew), jnp.int32)
    twos = (amount - 1) // 2
    source_of, sink = lengths[1:1 + 2 * twos:2], lengths[2:2 + 2 * twos:2]
    room = jnp.minimum(source_of - 1, limit - sink)
    shifted = jax.random.randint(jax.random.fold_in(rng, 1), (twos,), 0, 1 << 20) % (room + 1)
    lengths = lengths.at[1:1 + 2 * twos:2].set(source_of - shifted).at[2:2 + 2 * twos:2].set(sink + shifted)
    return lengths[jax.random.permutation(jax.random.fold_in(rng, 2), amount)]


def normal_values(key, shape, width, most, shards=(), held_as=jnp.bfloat16):
    gain = level_of(key, shape, shards, -0.22, 0.18) if shards else 1.0
    values = jax.random.normal(key, shape, jnp.float32) * width * gain
    return jnp.minimum(jnp.maximum(values, -most), most).astype(held_as)


def setup_inputs(seed: int = 0) -> dict:
    key_of = jax.random.split(jax.random.key(seed), 14)
    tokens = normal_values(key_of[0], (RANKS, MB, SLOT, D), 1.0, 6.0, ((0, 4), (2, 4)))
    images = jax.vmap(lambda own: jnp.searchsorted(jnp.cumsum(ragged(own, IMAGES, SLOT, LONGEST, 2)), jnp.arange(SLOT), side="right"))(jax.random.split(key_of[1], RANKS * MB)).reshape((RANKS, MB, SLOT)).astype(jnp.int32)
    norm_gain = jnp.clip(1.0 + 0.1 * jax.random.normal(key_of[2], (LAYERS, 2, D), jnp.float32), 0.5, 1.5)
    norm_shift = normal_values(key_of[3], (LAYERS, 2, D), 0.3, 1.5, ((0, 2),), jnp.float32)
    input_bias = normal_values(key_of[4], (LAYERS, 2, D), 0.5, 2.5, ((0, 2), (2, 4)), jnp.float32)
    project_in = normal_values(key_of[5], (LAYERS, 3, D, D), D ** -0.5, 0.21875, ((0, 2), (3, 4)))
    project_out = normal_values(key_of[6], (LAYERS, D, D), (max(D // 64, 1)) ** -0.5, 1.75, ((0, 2), (1, 4)))
    branch_bias = normal_values(key_of[7], (LAYERS, 2, D), 0.3, 1.5, ((0, 2),), jnp.float32)
    layer_scale = jnp.clip(jnp.exp(math.log(2.0) - 1.3862944 * jax.random.uniform(key_of[8], (LAYERS, 2, D), jnp.float32) ** level_of(key_of[8], (LAYERS, 2, D), ((0, 2),), -0.2, 0.2)), 0.5, 2.0)
    expand_bias = normal_values(key_of[9], (LAYERS, FF), 0.3, 1.5, ((0, 2), (1, 4)), jnp.float32)
    expand_weight = normal_values(key_of[10], (LAYERS, D, FF), D ** -0.5, 0.21875, ((0, 2), (2, 4)))
    reduce_weight = normal_values(key_of[11], (LAYERS, FF, D), FF ** -0.5, 0.109375, ((0, 2), (1, 4)))
    cotangent = normal_values(key_of[12], (RANKS, MB, SLOT, D), 1.0, 6.0, ((0, 4), (2, 4)))
    return {"tokens": tokens, "images": images, "norm_gain": norm_gain, "norm_shift": norm_shift, "input_bias": input_bias, "project_in": project_in, "project_out": project_out, "branch_bias": branch_bias, "layer_scale": layer_scale, "expand_bias": expand_bias, "expand_weight": expand_weight, "reduce_weight": reduce_weight, "cotangent": cotangent}


@jax.custom_vjp
def low(v):
    return lax.optimization_barrier(v.astype(jnp.bfloat16)).astype(jnp.float32)

@jax.custom_vjp
def low_back(v):
    return v

def low_keep(v):
    return (low(v), None)

def low_pass(kept, grad):
    return (grad,)

def back_keep(v):
    return (v, None)

def back_low(kept, grad):
    return (low(grad),)
low.defvjp(low_keep, low_pass)
low_back.defvjp(back_keep, back_low)
norm_eps = 1e-06
masked_score = -1e+30
highest = lax.Precision.HIGHEST

def matmul(left, right):
    return jnp.dot(left, right, precision=highest, preferred_element_type=jnp.float32)

def normalize(stream, gain_row, shift_row):
    center = stream - lax.optimization_barrier(jnp.mean(stream, axis=-1, keepdims=True))
    inv_dev = lax.rsqrt(lax.optimization_barrier(jnp.mean(center * center, axis=-1, keepdims=True)) + norm_eps)
    return center * inv_dev * gain_row + shift_row

def attention_block(query_block, seg_block, key_heads, value_heads, segment_ids):
    scores = jnp.einsum('qhc,khc->hqk', query_block, key_heads, precision=highest) * HEAD_DIM ** (-0.5)
    same_image = (seg_block[:, None] == segment_ids[None, :])[None]
    scores = low_back(jnp.where(same_image, scores, masked_score))
    row_top = lax.optimization_barrier(jnp.max(scores, axis=-1, keepdims=True))
    logsum = row_top + jnp.log(lax.optimization_barrier(jnp.sum(jnp.exp(scores - row_top), axis=-1, keepdims=True)))
    attn_probs = low(jnp.exp(scores - logsum))
    mixed = jnp.einsum('hqk,khc->qhc', attn_probs, value_heads, precision=highest)
    return mixed.reshape(query_block.shape[0], HEADS * HEAD_DIM)

def attention(query_rows, key_rows, value_rows, segment_ids):
    total_rows = query_rows.shape[0]
    block_rows = min(512, total_rows)
    block_count = total_rows // block_rows
    queries = query_rows.reshape(block_count, block_rows, HEADS, HEAD_DIM)
    key_heads = key_rows.reshape(total_rows, HEADS, HEAD_DIM)
    value_heads = value_rows.reshape(total_rows, HEADS, HEAD_DIM)
    seg_blocks = segment_ids.reshape(block_count, block_rows)
    checked = jax.checkpoint(attention_block)

    def block_step(item_pair):
        return checked(item_pair[0], item_pair[1], key_heads, value_heads, segment_ids)
    mixed = lax.map(block_step, (queries, seg_blocks))
    return mixed.reshape(total_rows, HEADS * HEAD_DIM)

def layer_ref(stream, segment_ids, norm_gain, norm_shift, input_bias, project_in, project_out, branch_bias, layer_scale, expand_bias, expand_weight, reduce_weight):
    normed = low(normalize(stream, norm_gain[0], norm_shift[0]))
    query_rows = low_back(low(matmul(normed, project_in[0]) + input_bias[0]))
    key_rows = low_back(low(matmul(normed, project_in[1])))
    value_rows = low_back(low(matmul(normed, project_in[2]) + input_bias[1]))
    mixed = low_back(low(attention(query_rows, key_rows, value_rows, segment_ids)))
    branch_one = low_back(matmul(mixed, project_out))
    middle = stream + layer_scale[0] * (branch_one + branch_bias[0])
    normed_two = low(normalize(middle, norm_gain[1], norm_shift[1]))
    hidden = low_back(matmul(normed_two, expand_weight) + expand_bias)
    active = low(jax.nn.gelu(hidden, approximate=False))
    branch_two = low_back(matmul(active, reduce_weight))
    return middle + layer_scale[1] * (branch_two + branch_bias[1])

def reference(tokens, images, norm_gain, norm_shift, input_bias, project_in, project_out, branch_bias, layer_scale, expand_bias, expand_weight, reduce_weight, cotangent):
    params = tuple((member.astype(jnp.float32) for member in (norm_gain, norm_shift, input_bias, project_in, project_out, branch_bias, layer_scale, expand_bias, expand_weight, reduce_weight)))
    slot_count = RANKS * MB
    streams = tokens.reshape(slot_count, SLOT, D).astype(jnp.float32)
    segments = images.reshape(slot_count, SLOT).astype(jnp.int32)
    pulls = cotangent.reshape(slot_count, SLOT, D).astype(jnp.float32)

    def two_layers(layer_params, stream, segment_ids):
        first_out = layer_ref(stream, segment_ids, *[member[0] for member in layer_params])
        first_out = low_back(low(first_out))
        return layer_ref(first_out, segment_ids, *[member[1] for member in layer_params])

    def slot_step(running, item_triple):
        stream, segment_ids, pull_rows = item_triple

        def forward(layer_params, inputs):
            return two_layers(layer_params, inputs, segment_ids)
        output, backward = jax.vjp(forward, params, stream)
        grad_params, grad_stream = backward(pull_rows)
        running = jax.tree.map(jnp.add, running, grad_params)
        return (running, (output.astype(jnp.bfloat16), grad_stream.astype(jnp.bfloat16)))
    zero_grads = tuple((jnp.zeros_like(member) for member in params))
    totals, outputs = lax.scan(slot_step, zero_grads, (streams, segments, pulls))
    full_shape = (RANKS, MB, SLOT, D)
    return (outputs[0].reshape(full_shape), outputs[1].reshape(full_shape), totals[0], totals[1], totals[2], totals[3], totals[4], totals[5], totals[6], totals[7], totals[8], totals[9])
```

```python
import functools
import jax
import jax.numpy as jnp
from jax import lax
from jax.experimental import pallas as pl
from jax.experimental.pallas import tpu as pltpu
from jax.sharding import PartitionSpec as P

HEAD_DIM = 64
LANES = 128
norm_eps = 1e-06
masked_score = -1e30
root_half = 0.7071067811865476
inv_root_tau = 0.3989422804014327
f32 = jnp.float32
bf16 = jnp.bfloat16


def swap(x, axis, mask):
    n = lax.axis_size(axis)
    return lax.ppermute(x, axis, [(i, i ^ mask) for i in range(n)])


def swap_chip(x):
    return swap(x, "head", 2)


def swap_core(x):
    return swap(x, "head", 1)


def swap_section(x):
    return swap(x, "section", 1)


def dot(a, b):
    return jnp.dot(a, b, preferred_element_type=f32)


def dot_t(a, b):
    return lax.dot_general(a, b, (((1,), (1,)), ((), ())), preferred_element_type=f32)


def dot_rows(a, b):
    return lax.dot_general(a, b, (((0,), (0,)), ((), ())), preferred_element_type=f32)


def normalize(stream, gain, shift):
    center = stream - jnp.mean(stream, axis=-1, keepdims=True)
    inv_dev = lax.rsqrt(jnp.mean(center * center, axis=-1, keepdims=True) + norm_eps)
    unit = center * inv_dev
    return (unit * gain + shift).astype(bf16), unit, inv_dev


def normalize_back(grad, unit, inv_dev, gain):
    scaled = grad * gain
    inner = scaled - jnp.mean(scaled, axis=-1, keepdims=True)
    inner = inner - unit * jnp.mean(scaled * unit, axis=-1, keepdims=True)
    return inv_dev * inner, jnp.sum(grad * unit, axis=0), jnp.sum(grad, axis=0)


def attn_fwd_kernel(qr, kr, q_ref, k_ref, v_ref, sq_ref, sk_ref, o_ref, lse_ref, m_ref, l_ref, acc_ref, *, qb, kb):
    pairs = q_ref.shape[1] // LANES
    nk = k_ref.shape[0] // kb
    i = pl.program_id(0)
    m_ref[...] = jnp.full_like(m_ref, -3e38)
    l_ref[...] = jnp.zeros_like(l_ref)
    acc_ref[...] = jnp.zeros_like(acc_ref)
    lane = lax.broadcasted_iota(jnp.int32, (qb, LANES), 1)
    lo, hi = qr[0, i], qr[1, i]
    for j in range(nk):
        @pl.when(jnp.logical_and(kr[0, j] <= hi, kr[1, j] >= lo))
        def _():
            bias = jnp.where(sk_ref[pl.ds(j * kb, kb), :] == sq_ref[...], 0.0, masked_score)
            for p in range(pairs):
                cols = pl.ds(p * LANES, LANES)
                kblk = k_ref[pl.ds(j * kb, kb), cols]
                vblk = v_ref[pl.ds(j * kb, kb), cols]
                qblk = q_ref[:, cols]
                for e in range(2):
                    h = 2 * p + e
                    qm = jnp.where((lane < HEAD_DIM) == (e == 0), qblk, jnp.zeros_like(qblk))
                    s = dot_t(kblk, qm) + bias
                    top = m_ref[h:h + 1, :]
                    new = jnp.maximum(top, jnp.max(s, axis=0, keepdims=True))
                    alpha = jnp.exp(top - new)
                    pr = jnp.exp(s - new)
                    l_ref[h:h + 1, :] = l_ref[h:h + 1, :] * alpha + jnp.sum(pr, axis=0, keepdims=True)
                    m_ref[h:h + 1, :] = new
                    ov = dot_rows(vblk, pr.astype(bf16))
                    rows = pl.ds(h * HEAD_DIM, HEAD_DIM)
                    acc_ref[rows, :] = acc_ref[rows, :] * alpha + ov[e * HEAD_DIM:(e + 1) * HEAD_DIM, :]
    for h in range(2 * pairs):
        rows = pl.ds(h * HEAD_DIM, HEAD_DIM)
        acc_ref[rows, :] = acc_ref[rows, :] / l_ref[h:h + 1, :]
    o_ref[...] = acc_ref[...].T.astype(bf16)
    lse_ref[...] = m_ref[...] + jnp.log(jnp.maximum(l_ref[...], 1e-37))


def attend(q, k, v, seg_q, seg_k, qb=128, kb=384):
    rows, width = q.shape
    keys = k.shape[0]
    heads = width // HEAD_DIM
    qs = seg_q.reshape(rows // qb, qb)
    ks = seg_k.reshape(keys // kb, kb)
    qr = jnp.stack([qs[:, 0], qs[:, -1]])
    kr = jnp.stack([ks[:, 0], ks[:, -1]])
    return pl.pallas_call(
        functools.partial(attn_fwd_kernel, qb=qb, kb=kb),
        grid_spec=pltpu.PrefetchScalarGridSpec(
            num_scalar_prefetch=2,
            grid=(rows // qb,),
            in_specs=[
                pl.BlockSpec((qb, width), lambda i, *_: (i, 0)),
                pl.BlockSpec((keys, width), lambda i, *_: (0, 0)),
                pl.BlockSpec((keys, width), lambda i, *_: (0, 0)),
                pl.BlockSpec((1, qb), lambda i, *_: (0, i)),
                pl.BlockSpec((keys, 1), lambda i, *_: (0, 0)),
            ],
            out_specs=[
                pl.BlockSpec((qb, width), lambda i, *_: (i, 0)),
                pl.BlockSpec((8, qb), lambda i, *_: (0, i)),
            ],
            scratch_shapes=[
                pltpu.VMEM((8, qb), f32),
                pltpu.VMEM((8, qb), f32),
                pltpu.VMEM((width, qb), f32),
            ],
        ),
        out_shape=[
            jax.ShapeDtypeStruct((rows, width), bf16),
            jax.ShapeDtypeStruct((8, rows), f32),
        ],
        name="attn_fwd",
    )(qr, kr, q, k, v, seg_q.reshape(1, rows), seg_k.reshape(keys, 1))


def attn_bwd_kernel(qr, kr, q_ref, k_ref, v_ref, g_ref, o_ref, lse_ref, sq_ref, sk_ref, gq_ref, gk_ref, gv_ref, gqa_ref, *, qb, kb):
    pairs = q_ref.shape[1] // LANES
    nk = k_ref.shape[0] // kb
    i = pl.program_id(0)

    @pl.when(i == 0)
    def _():
        gk_ref[...] = jnp.zeros_like(gk_ref)
        gv_ref[...] = jnp.zeros_like(gv_ref)

    gqa_ref[...] = jnp.zeros_like(gqa_ref)
    lane = lax.broadcasted_iota(jnp.int32, (qb, LANES), 1)
    picks = lax.broadcasted_iota(jnp.int32, (8, LANES), 1)
    lo, hi = qr[0, i], qr[1, i]
    deltas = []
    for p in range(pairs):
        cols = pl.ds(p * LANES, LANES)
        prod = g_ref[:, cols].astype(f32) * o_ref[:, cols].astype(f32)
        for e in range(2):
            pick = jnp.where((picks < HEAD_DIM) == (e == 0), 1.0, 0.0)
            both = lax.dot_general(pick, prod, (((1,), (1,)), ((), ())), precision=lax.Precision.HIGHEST, preferred_element_type=f32)
            deltas.append(both[0:1, :])
    for j in range(nk):
        @pl.when(jnp.logical_and(kr[0, j] <= hi, kr[1, j] >= lo))
        def _():
            krows = pl.ds(j * kb, kb)
            same = sk_ref[krows, :] == sq_ref[...]
            bias = jnp.where(same, 0.0, masked_score)
            for p in range(pairs):
                cols = pl.ds(p * LANES, LANES)
                kblk = k_ref[krows, cols]
                vblk = v_ref[krows, cols]
                qblk = q_ref[:, cols]
                gblk = g_ref[:, cols]
                gk_new, gv_new, gq_new = 0.0, 0.0, 0.0
                for e in range(2):
                    h = 2 * p + e
                    mine = (lane < HEAD_DIM) == (e == 0)
                    qm = jnp.where(mine, qblk, jnp.zeros_like(qblk))
                    gm = jnp.where(mine, gblk, jnp.zeros_like(gblk))
                    s = dot_t(kblk, qm) + bias
                    pr = jnp.exp(s - lse_ref[h:h + 1, :])
                    gp = dot_t(vblk, gm)
                    gs = (pr * (gp - deltas[h])).astype(bf16)
                    gv_new = gv_new + dot(pr.astype(bf16), gm)
                    gk_new = gk_new + dot(gs, qm)
                    gq_new = gq_new + jnp.where(mine, dot_rows(gs, kblk), 0.0)
                gv_ref[krows, cols] += gv_new
                gk_ref[krows, cols] += gk_new
                gqa_ref[:, cols] += gq_new
    gq_ref[...] = (gqa_ref[...] * HEAD_DIM ** -0.5).astype(bf16)


def attend_back(q, k, v, seg_q, seg_k, g, o, lse, qb=128, kb=384):
    rows, width = q.shape
    keys = k.shape[0]
    qs = seg_q.reshape(rows // qb, qb)
    ks = seg_k.reshape(keys // kb, kb)
    qr = jnp.stack([qs[:, 0], qs[:, -1]])
    kr = jnp.stack([ks[:, 0], ks[:, -1]])
    qspec = pl.BlockSpec((qb, width), lambda i, *_: (i, 0))
    kspec = pl.BlockSpec((keys, width), lambda i, *_: (0, 0))
    return pl.pallas_call(
        functools.partial(attn_bwd_kernel, qb=qb, kb=kb),
        grid_spec=pltpu.PrefetchScalarGridSpec(
            num_scalar_prefetch=2,
            grid=(rows // qb,),
            in_specs=[
                qspec, kspec, kspec, qspec, qspec,
                pl.BlockSpec((8, qb), lambda i, *_: (0, i)),
                pl.BlockSpec((1, qb), lambda i, *_: (0, i)),
                pl.BlockSpec((keys, 1), lambda i, *_: (0, 0)),
            ],
            out_specs=[qspec, kspec, kspec],
            scratch_shapes=[pltpu.VMEM((qb, width), f32)],
        ),
        out_shape=[
            jax.ShapeDtypeStruct((rows, width), bf16),
            jax.ShapeDtypeStruct((keys, width), f32),
            jax.ShapeDtypeStruct((keys, width), f32),
        ],
        name="attn_bwd",
    )(qr, kr, q, k, v, g, o, lse, seg_q.reshape(1, rows), seg_k.reshape(keys, 1))


def gelu_parts(u):
    cdf = 0.5 * (1.0 + lax.erf(u * root_half))
    slope = cdf + u * inv_root_tau * jnp.exp(-0.5 * u * u)
    return (u * cdf).astype(bf16), slope.astype(bf16)


def layer_forward(stream, segs, w):
    seg_q, seg_k = segs
    width = w["out"].shape[0]
    n1, unit1, inv1 = normalize(stream, w["gain"][0], w["shift"][0])
    n1 = jnp.concatenate([n1, swap_chip(n1)])
    qkv = (dot(n1, w["in"]) + w["in_bias"]).astype(bf16)
    own = n1.shape[0] // 2
    q = qkv[:, :width] * jnp.bfloat16(HEAD_DIM ** -0.5)
    kv = qkv[:, width:]
    kv = jnp.concatenate([kv, swap_core(kv)])
    k, v = kv[:, :width], kv[:, width:]
    mixed, lse = attend(q, k, v, seg_q, seg_k)
    branch1 = dot(mixed[:own], w["out"]) + swap_chip(dot(mixed[own:], w["out"]).astype(bf16)).astype(f32)
    branch1 = branch1 + w["bias"][0]
    middle = stream + w["scale"][0] * branch1
    n2, unit2, inv2 = normalize(middle, w["gain"][1], w["shift"][1])
    n2r = swap_chip(n2)
    act_o, slope_o = gelu_parts(dot(n2, w["expand"]) + w["expand_bias"])
    act_r, slope_r = gelu_parts(dot(n2r, w["expand"]) + w["expand_bias"])
    back = swap_chip(dot(act_r, w["reduce"]).astype(bf16))
    branch2 = dot(act_o, w["reduce"]) + back.astype(f32) + w["bias"][1]
    result = middle + w["scale"][1] * branch2
    kept = (n1, unit1, inv1, q, k, v, mixed, lse, branch1, n2, n2r, unit2, inv2, act_o, slope_o, act_r, slope_r, branch2)
    return result, kept


def layer_backward(g_out, segs, w, kept):
    n1, unit1, inv1, q, k, v, mixed, lse, branch1, n2, n2r, unit2, inv2, act_o, slope_o, act_r, slope_r, branch2 = kept
    seg_q, seg_k = segs
    own = n2.shape[0]
    g_scale2 = jnp.sum(g_out * branch2, axis=0)
    g_bias2 = jnp.sum(g_out, axis=0) * w["scale"][1]
    gb2 = (g_out * w["scale"][1]).astype(bf16)
    gb2r = swap_chip(gb2)
    gh_o = (dot_t(gb2, w["reduce"]) * slope_o.astype(f32)).astype(bf16)
    gh_r = (dot_t(gb2r, w["reduce"]) * slope_r.astype(f32)).astype(bf16)
    back = swap_chip(dot_t(gh_r, w["expand"]).astype(bf16))
    g_n2 = dot_t(gh_o, w["expand"]) + back.astype(f32)
    g_reduce = dot_rows(act_o, gb2) + dot_rows(act_r, gb2r)
    g_expand = dot_rows(n2, gh_o) + dot_rows(n2r, gh_r)
    g_expand_bias = jnp.sum(gh_o.astype(f32), axis=0) + jnp.sum(gh_r.astype(f32), axis=0)
    back2, g_gain2, g_shift2 = normalize_back(g_n2, unit2, inv2, w["gain"][1])
    g_mid = g_out + back2
    g_scale1 = jnp.sum(g_mid * branch1, axis=0)
    g_bias1 = jnp.sum(g_mid, axis=0) * w["scale"][0]
    gb1 = (g_mid * w["scale"][0]).astype(bf16)
    gb1 = jnp.concatenate([gb1, swap_chip(gb1)])
    g_out_w = dot_rows(mixed, gb1)
    g_mixed = dot_t(gb1, w["out"]).astype(bf16)
    gq, gk, gv = attend_back(q, k, v, seg_q, seg_k, g_mixed, mixed, lse)
    half = 2 * own
    other = swap_core(jnp.concatenate([gk[half:], gv[half:]], axis=1).astype(bf16))
    gkv = (jnp.concatenate([gk[:half], gv[:half]], axis=1) + other.astype(f32)).astype(bf16)
    g_qkv = jnp.concatenate([gq, gkv], axis=1)
    g_in_w = dot_rows(n1, g_qkv)
    g_in_bias = jnp.sum(g_qkv.astype(f32), axis=0)
    back = swap_chip(dot_t(g_qkv[own:], w["in"]).astype(bf16))
    g_n1 = dot_t(g_qkv[:own], w["in"]) + back.astype(f32)
    back1, g_gain1, g_shift1 = normalize_back(g_n1, unit1, inv1, w["gain"][0])
    g_in = g_mid + back1
    small = jnp.stack([g_gain1, g_gain2, g_shift1, g_shift2, g_bias1, g_bias2, g_scale1, g_scale2])
    large = {"in": g_in_w, "in_bias": g_in_bias, "out": g_out_w, "expand": g_expand, "expand_bias": g_expand_bias, "reduce": g_reduce}
    return g_in, large, small


def body(tokens, images, norm_gain, norm_shift, input_bias, project_in, project_out, branch_bias, layer_scale, expand_bias, expand_weight, reduce_weight, cotangent):
    section = lax.axis_index("section")
    head = lax.axis_index("head")
    core = head % 2
    first = section == 0
    quarter = project_in.shape[3]
    own = {
        "in": project_in[0].transpose(1, 0, 2).reshape(project_in.shape[2], -1),
        "out": project_out[0],
        "expand": expand_weight[0],
        "reduce": reduce_weight[0],
        "small": jnp.concatenate([norm_gain[0], norm_shift[0], branch_bias[0], layer_scale[0]]),
        "vec": jnp.concatenate([input_bias[0].reshape(-1), expand_bias[0]]),
    }
    other = jax.tree.map(swap_section, own)
    layers = []
    for layer in range(2):
        mine = first if layer == 0 else jnp.logical_not(first)
        a = jax.tree.map(lambda x, y: jnp.where(mine, x, y), own, other)
        b = {name: swap_core(a[name]) for name in ("in", "out", "expand", "reduce", "vec")}
        parts = []
        even = {name: jnp.where(core == 0, a[name], b[name]) for name in ("in", "out", "vec")}
        odd = {name: jnp.where(core == 0, b[name], a[name]) for name in ("in", "out", "vec")}
        for j in range(3):
            cols = slice(j * quarter, (j + 1) * quarter)
            parts += [even["in"][:, cols], odd["in"][:, cols]]
        zero = jnp.zeros((2 * quarter,), f32)
        w = {
            "in": jnp.concatenate(parts, axis=1),
            "out": jnp.concatenate([even["out"], odd["out"]]),
            "expand": jnp.concatenate([a["expand"], b["expand"]], axis=1),
            "reduce": jnp.concatenate([a["reduce"], b["reduce"]]),
            "gain": a["small"][0:2], "shift": a["small"][2:4], "bias": a["small"][4:6], "scale": a["small"][6:8],
            "in_bias": jnp.concatenate([even["vec"][:quarter], odd["vec"][:quarter], zero, even["vec"][quarter:2 * quarter], odd["vec"][quarter:2 * quarter]]),
            "expand_bias": jnp.concatenate([a["vec"][2 * quarter:], b["vec"][2 * quarter:]]),
        }
        layers.append(w)
    pieces = lax.dynamic_index_in_dim(images[0], section, 0, keepdims=False).reshape(lax.axis_size("head"), -1)
    order = [lax.dynamic_index_in_dim(pieces, head ^ mask, 0, keepdims=False) for mask in (0, 2, 1, 3)]
    segs = (jnp.concatenate(order[:2]), jnp.concatenate(order))
    stream = lax.dynamic_index_in_dim(tokens[0], section, 0, keepdims=False).astype(f32)
    result, kept0 = layer_forward(stream, segs, layers[0])
    result, kept1 = layer_forward(result.astype(bf16).astype(f32), segs, layers[1])
    final_tokens = result.astype(bf16)
    g_out = lax.dynamic_index_in_dim(cotangent[0], section, 0, keepdims=False).astype(f32)
    g_in, large1, small1 = layer_backward(g_out, segs, layers[1], kept1)
    g_in, large0, small0 = layer_backward(g_in.astype(bf16).astype(f32), segs, layers[0], kept0)
    grad_tokens = g_in.astype(bf16)

    def by_core(large):
        mine, theirs = {}, {}
        w = 2 * quarter
        mine["in"] = jnp.stack([large["in"][:, j * w:j * w + quarter] for j in range(3)])
        theirs["in"] = jnp.stack([large["in"][:, j * w + quarter:(j + 1) * w] for j in range(3)])
        mine["in_bias"] = jnp.stack([large["in_bias"][j * w:j * w + quarter] for j in (0, 2)])
        theirs["in_bias"] = jnp.stack([large["in_bias"][j * w + quarter:(j + 1) * w] for j in (0, 2)])
        mine["out"], theirs["out"] = jnp.split(large["out"], 2)
        for name in ("in", "in_bias", "out"):
            even, odd = mine[name], theirs[name]
            mine[name], theirs[name] = jnp.where(core == 0, even, odd), jnp.where(core == 0, odd, even)
        for name, axis in (("expand", 1), ("expand_bias", 0), ("reduce", 0)):
            mine[name], theirs[name] = jnp.split(large[name], 2, axis=axis)
        return {name: mine[name] + swap_core(theirs[name].astype(bf16)).astype(f32) for name in mine}

    large0, large1 = by_core(large0), by_core(large1)
    total = {}
    for name in large0:
        send = jnp.where(first, large1[name], large0[name]).astype(bf16)
        keep = jnp.where(first, large0[name], large1[name])
        total[name] = (keep + swap_section(send).astype(f32)).astype(bf16)
    total = {name: part.astype(f32) for name, part in lax.psum(total, "dp").items()}
    small = lax.psum(jnp.stack([small0, small1]), ("section", "head", "dp"))
    small = lax.dynamic_index_in_dim(small, section, 0, keepdims=False)
    return (
        final_tokens[None, None],
        grad_tokens[None, None],
        small[None, 0:2],
        small[None, 2:4],
        total["in_bias"][None],
        total["in"][None],
        total["out"][None],
        small[None, 4:6],
        small[None, 6:8],
        total["expand_bias"][None],
        total["expand"][None],
        total["reduce"][None],
    )


def solution(mesh):
    return jax.shard_map(
        body,
        mesh=mesh,
        in_specs=(
            P("dp", None, "head", None),
            P("dp", None, None),
            P("section", None, None),
            P("section", None, None),
            P("section", None, "head"),
            P("section", None, None, "head"),
            P("section", "head", None),
            P("section", None, None),
            P("section", None, None),
            P("section", "head"),
            P("section", None, "head"),
            P("section", "head", None),
            P("dp", None, "head", None),
        ),
        out_specs=(
            P("dp", "section", "head", None),
            P("dp", "section", "head", None),
            P("section", None, None),
            P("section", None, None),
            P("section", None, "head"),
            P("section", None, None, "head"),
            P("section", "head", None),
            P("section", None, None),
            P("section", None, None),
            P("section", "head"),
            P("section", None, "head"),
            P("section", "head", None),
        ),
        check_vma=False,
    )
```
